32 devices in a mesh: tm: 8 (over z, x), pix: 4 (over y, core).
Axes of the slice: x: 2, y: 2, z: 4, core: 2. Of those that a mesh axis runs over, the one named last changes fastest.
Arguments:
- movie: bfloat16 [8, 2048, 2048], P('tm', 'pix'), may hold values from -6 to 6
- shifts: int32 [8, 16, 16, 2], P('tm', 'pix'), may hold values from -16 to 16
- footprints: bfloat16 [4, 256, 64, 4096], P('pix', 'tm'), may hold values from -0.0234375 to 0.0234375
- neuron_ids: int32 [4, 256, 64], P('pix', 'tm'), may hold values from 0 to 4095
Outputs:
- traces: float32 [4096, 8], P(('tm', 'pix'))
The draws below stay inside these ranges and needn't reach their ends.
All inputs are finite; a program needn't handle non-finite values.
Results may differ from the reference program's by a relative error of at most 0.0029.
Values may be sent and summed in bfloat16 or wider, within the bound.
A program may use at most 128 MiB of HBM per device.

```python
import jax
import jax.numpy as jnp
from jax import lax

HEIGHT = 2048
WIDTH = 2048
TILE = 128
MAXSHIFT = 16
PATCH = 64
FOOT_COLS = 64
HOMES = 4
FRAMES = 8
PATCHES = 1024
NEURONS = 4096
N_PIX = 4


def draw_neuron_ids(key, part):
    rows_p = HEIGHT // PATCH
    cols_p = WIDTH // PATCH
    count = rows_p * cols_p
    key_rows, key_cols, key_home, key_far, key_pick = jax.random.split(key, 5)
    step_rows = jax.random.randint(key_rows, (count, FOOT_COLS), -1, 2)
    step_cols = jax.random.randint(key_cols, (count, FOOT_COLS), -1, 2)
    homes = jax.random.randint(key_home, (count, FOOT_COLS), 0, HOMES)
    far_labels = jax.random.randint(key_far, (count, FOOT_COLS), 0, NEURONS)
    far_pick = jax.random.randint(key_pick, (count, FOOT_COLS), 0, 4)
    places = jnp.arange(count, dtype=jnp.int32)
    target_rows = jnp.clip(places[:, None] // cols_p + step_rows, 0, rows_p - 1)
    target_cols = jnp.clip(places[:, None] % cols_p + step_cols, 0, cols_p - 1)
    near_labels = (target_rows * cols_p + target_cols) * HOMES + homes
    labels = jnp.where(far_pick == 0, far_labels, near_labels)
    labels = labels.at[0, 0].set(0)
    labels = labels.at[count - 1, 0].set(NEURONS - 1)
    return labels.astype(jnp.int32).reshape(N_PIX, count // N_PIX, FOOT_COLS)


def set_ends(array, stream_key, least, high):
    extent = array.shape
    place = [jax.random.randint(jax.random.fold_in(stream_key, axis), (), 0, extent[axis]) for axis in range(len(extent))]
    array = array.at[tuple(place)].set(least)
    longest = extent.index(max(extent))
    place[longest] = (place[longest] + 1) % extent[longest]
    return array.at[tuple(place)].set(high)


def levels(rng, dims, cuts, least, largest):
    level = 1.0
    for position, parts in cuts:
        draws = jax.random.uniform(jax.random.fold_in(jax.random.fold_in(rng, 6), position), (parts,), jnp.float32, least / len(cuts), largest / len(cuts))
        level = level * jnp.repeat(jnp.exp(draws), dims[position] // parts).reshape((-1,) + (1,) * (len(dims) - 1 - position))
    return level


def gaussian(rng, extent, scale, bound, cuts=(), kind=jnp.bfloat16):
    result = jax.random.normal(rng, extent, jnp.float32) * scale
    if len(cuts) > 0:
        result = levels(rng, extent, cuts, -0.22, 0.18) * result
    return jnp.clip(result, min=-bound, max=bound).astype(kind)


def setup_inputs(seed: int = 0) -> dict:
    seeds = jax.random.split(jax.random.key(seed), 5)
    return {
        "movie": gaussian(seeds[0], (FRAMES, HEIGHT, WIDTH), 1.0, 6.0, ((0, 8), (1, 4))),
        "shifts": set_ends(jax.random.randint(seeds[1], (FRAMES, HEIGHT // TILE, WIDTH // TILE, 2), 0 - MAXSHIFT, MAXSHIFT + 1), jax.random.fold_in(seeds[1], 1), 0 - MAXSHIFT, MAXSHIFT).astype(jnp.int32),
        "footprints": gaussian(seeds[2], (N_PIX, PATCHES // N_PIX, FOOT_COLS, PATCH * PATCH), (16 * PATCH * PATCH) ** -0.5, 0.0234375, ((0, 4), (1, 8))),
        "neuron_ids": draw_neuron_ids(jax.random.fold_in(seeds[4], 71), 0),
    }


pixel_sigma = 3.0
frame_sigma = 4.0


def gauss_table(count, sigma):
    places = jnp.arange(count).astype(jnp.float32)
    apart = places[:, None] - places[None, :]
    weights = jnp.exp(-apart * apart / (2.0 * sigma * sigma))
    return weights / jnp.sum(weights, axis=1, keepdims=True)


def rounded(values):
    return lax.optimization_barrier(values.astype(jnp.bfloat16)).astype(jnp.float32)


def shift_frame(frame, shift):
    padded = jnp.pad(frame, MAXSHIFT)
    row_index = jnp.arange(HEIGHT, dtype=jnp.int32)[:, None] + jnp.zeros((1, WIDTH), jnp.int32)
    col_index = jnp.arange(WIDTH, dtype=jnp.int32)[None, :] + jnp.zeros((HEIGHT, 1), jnp.int32)
    vertical = shift[row_index // TILE, col_index // TILE, 0]
    horizontal = shift[row_index // TILE, col_index // TILE, 1]
    return padded[row_index + MAXSHIFT + vertical, col_index + MAXSHIFT + horizontal]


def reference(movie, shifts, footprints, neuron_ids):
    registered = lax.map(lambda pair: shift_frame(pair[0], pair[1]), (movie, shifts))
    patch_table = rounded(gauss_table(PATCH, pixel_sigma))
    time_table = rounded(gauss_table(FRAMES, frame_sigma))
    rows_p = HEIGHT // PATCH
    cols_p = WIDTH // PATCH
    blocks = footprints.reshape(rows_p, cols_p, FOOT_COLS, PATCH, PATCH)

    def one_row(item):
        index, foot_block = item
        strip = lax.dynamic_slice_in_dim(registered, index * PATCH, PATCH, axis=1)
        pixels = strip.reshape(FRAMES, PATCH, cols_p, PATCH).astype(jnp.float32)
        along_rows = rounded(jnp.einsum("ij,fjbc->fibc", patch_table, pixels))
        along_cols = rounded(jnp.einsum("fibj,cj->fibc", along_rows, patch_table))
        along_time = jnp.einsum("gf,fibc->gibc", time_table, along_cols)
        cleaned = rounded(pixels - along_time)
        return jnp.einsum("fibc,bkic->bkf", cleaned, foot_block.astype(jnp.float32))

    partials = lax.map(one_row, (jnp.arange(rows_p, dtype=jnp.int32), blocks))
    partials = partials.reshape(PATCHES * FOOT_COLS, FRAMES)
    return jax.ops.segment_sum(partials, neuron_ids.reshape(-1), num_segments=NEURONS)
```

```python
import jax
import jax.numpy as jnp
import ml_dtypes
import numpy as np
from jax import lax
from jax.experimental import pallas as pl
from jax.experimental.pallas import tpu as pltpu
from jax.sharding import PartitionSpec as P

TILE = 128
MAXSHIFT = 16
PATCH = 64
NEURONS = 4096
LANES = 128
GROUP = 4


pixel_sigma = 3.0
frame_sigma = 4.0


def gauss_table(count, sigma):
    places = np.arange(count).astype(np.float32)
    apart = places[:, None] - places[None, :]
    weights = np.exp(-apart * apart / np.float32(2.0 * sigma * sigma)).astype(np.float32)
    table = weights / np.sum(weights, axis=1, keepdims=True, dtype=np.float32)
    return table.astype(ml_dtypes.bfloat16)


def halo(band):
    count = lax.axis_size("pix")
    up = [(i, i + 1) for i in range(count - 1)]
    down = [(i + 1, i) for i in range(count - 1)]
    before = lax.ppermute(band[-MAXSHIFT:], "pix", up)
    after = lax.ppermute(band[:MAXSHIFT], "pix", down)
    return before, after


def register_kernel(shift_ref, band_ref, before_ref, after_ref, out_ref, padded):
    rows, width = band_ref.shape
    across = width // TILE
    tall = rows + 2 * MAXSHIFT
    for j in (0, across + 1):
        padded[j] = jnp.zeros((tall, TILE), jnp.float32)
    for j in range(across):
        lanes = pl.ds(j * TILE, TILE)
        padded[j + 1, pl.ds(0, MAXSHIFT), :] = before_ref[:, lanes].astype(jnp.float32)
        padded[j + 1, pl.ds(MAXSHIFT, rows), :] = band_ref[:, lanes].astype(jnp.float32)
        padded[j + 1, pl.ds(rows + MAXSHIFT, MAXSHIFT), :] = after_ref[:, lanes].astype(jnp.float32)

    gap = lax.broadcasted_iota(jnp.int32, (2 * TILE, TILE), 0) - lax.broadcasted_iota(
        jnp.int32, (2 * TILE, TILE), 1
    )

    @pl.loop(0, rows // TILE)
    def _(a):
        for b in range(across):
            place = (a * across + b) * 2
            dy = shift_ref[place]
            dx = shift_ref[place + 1]
            left = dx < 0
            start = jnp.where(left, b, b + 1)
            at = pl.ds(a * TILE + MAXSHIFT + dy, TILE)
            window = jnp.concatenate([padded[start, at, :], padded[start + 1, at, :]], axis=1)
            pick = (gap == jnp.where(left, dx + TILE, dx)).astype(jnp.float32).astype(jnp.bfloat16)
            moved = jnp.dot(window.astype(jnp.bfloat16), pick, preferred_element_type=jnp.float32)
            out_ref[pl.ds(pl.multiple_of(a * TILE, TILE), TILE), b * TILE : (b + 1) * TILE] = moved.astype(
                jnp.bfloat16
            )


def register(band, before, after, shifts):
    rows, width = band.shape
    vmem = pl.BlockSpec(memory_space=pltpu.VMEM)
    return pl.pallas_call(
        register_kernel,
        out_shape=jax.ShapeDtypeStruct((rows, width), jnp.bfloat16),
        in_specs=[pl.BlockSpec(memory_space=pltpu.SMEM), vmem, vmem, vmem],
        out_specs=vmem,
        scratch_shapes=[pltpu.VMEM((width // TILE + 2, rows + 2 * MAXSHIFT, TILE), jnp.float32)],
        compiler_params=pltpu.CompilerParams(vmem_limit_bytes=24 << 20),
        name="register",
    )(shifts.reshape(-1), band, before, after)


def project_kernel(local, x_ref, foot_ref, ids_ref, row_ref, col_ref, mix_ref, out_ref):
    frames, side, cols = x_ref.shape
    half = row_ref.shape[0] // frames
    moved = x_ref[...].reshape(frames * side, cols)
    chunk = row_ref.shape[0]
    along_rows = jnp.concatenate(
        [
            jnp.dot(row_ref[...], moved[i : i + chunk], preferred_element_type=jnp.float32)
            for i in range(0, frames * side, chunk)
        ],
        axis=0,
    ).astype(jnp.bfloat16)
    along_cols = jnp.dot(along_rows, col_ref[...], preferred_element_type=jnp.float32).astype(jnp.bfloat16)
    patches = cols // side
    low = lax.broadcasted_iota(jnp.int32, (frames, LANES), 1) < side
    pieces = [[] for _ in range(patches)]
    for h in range(side // half):
        stack = [moved[f * side + h * half : f * side + (h + 1) * half] for f in range(frames)]
        stack += [along_cols[f * side + h * half : f * side + (h + 1) * half] for f in range(frames)]
        clean = jnp.dot(mix_ref[...], jnp.concatenate(stack, axis=0), preferred_element_type=jnp.float32)
        for i in range(half // 2):
            for j in range(cols // LANES):
                first = clean[2 * i * frames : (2 * i + 1) * frames, j * LANES : (j + 1) * LANES]
                second = clean[(2 * i + 1) * frames : (2 * i + 2) * frames, j * LANES : (j + 1) * LANES]
                pieces[2 * j].append(jnp.where(low, first, pltpu.roll(second, side, 1)))
                pieces[2 * j + 1].append(jnp.where(low, pltpu.roll(first, side, 1), second))
    pixels = jnp.concatenate([jnp.concatenate(p, axis=1) for p in pieces], axis=0).astype(jnp.bfloat16)
    blocks = foot_ref[...].reshape(patches * foot_ref.shape[1], side * side)
    product = lax.dot_general(pixels, blocks, (((1,), (1,)), ((), ())), preferred_element_type=jnp.float32)
    count = product.shape[1]
    owner_patch = lax.broadcasted_iota(jnp.int32, (frames, count), 1) // foot_ref.shape[1]
    partial = jnp.zeros((frames, count), jnp.float32)
    for p in range(patches):
        partial = jnp.where(owner_patch == p, product[p * frames : (p + 1) * frames], partial)
    ids = ids_ref[0]
    owner = jnp.broadcast_to(ids // local, (frames, count))
    within = ids % local
    onehot = (
        (lax.broadcasted_iota(jnp.int32, (local, count), 0) == within).astype(jnp.float32).astype(jnp.bfloat16)
    )
    total = None
    rest = partial
    for _ in range(3):
        piece = rest.astype(jnp.bfloat16).astype(jnp.float32)
        rest = rest - piece
        spread = jnp.concatenate(
            [jnp.where(owner == o, piece, 0.0) for o in range(NEURONS // local)], axis=0
        ).astype(jnp.bfloat16)
        term = lax.dot_general(spread, onehot, (((1,), (1,)), ((), ())), preferred_element_type=jnp.float32)
        total = term if total is None else total + term

    @pl.when(pl.program_id(0) == 0)
    def _():
        out_ref[...] = total

    @pl.when(pl.program_id(0) > 0)
    def _():
        out_ref[...] += total


def project(moved, footprints, labels, owners):
    frames, side, width = moved.shape
    steps = width // (GROUP * side)
    foot_cols = footprints.shape[1]
    local = NEURONS // owners
    base = gauss_table(side, pixel_sigma)
    time = gauss_table(frames, frame_sigma)
    full = GROUP * side
    eye = np.eye(GROUP, dtype=np.float32)
    row_table = np.kron(eye, base.astype(np.float32)).astype(ml_dtypes.bfloat16)
    col_table = np.kron(eye, base.astype(np.float32).T).astype(ml_dtypes.bfloat16)
    half = full // frames
    spots = np.eye(half, dtype=np.float32)
    keep = np.einsum("gf,rs->rgfs", np.eye(frames, dtype=np.float32), spots)
    blur = np.einsum("gf,rs->rgfs", time.astype(np.float32), spots)
    mix = np.concatenate([keep.reshape(full, full), -blur.reshape(full, full)], axis=1).astype(ml_dtypes.bfloat16)
    fixed = lambda shape: pl.BlockSpec(shape, lambda s: (0,) * len(shape))
    return pl.pallas_call(
        lambda *refs: project_kernel(local, *refs),
        out_shape=jax.ShapeDtypeStruct((owners * frames, local), jnp.float32),
        grid=(steps,),
        in_specs=[
            pl.BlockSpec((frames, side, full), lambda s: (0, 0, s)),
            pl.BlockSpec((GROUP, foot_cols, side * side), lambda s: (s, 0, 0)),
            pl.BlockSpec((1, 1, GROUP * foot_cols), lambda s: (s, 0, 0)),
            fixed(row_table.shape),
            fixed(col_table.shape),
            fixed(mix.shape),
        ],
        out_specs=fixed((owners * frames, local)),
        compiler_params=pltpu.CompilerParams(vmem_limit_bytes=40 << 20),
        name="project",
    )(
        moved,
        footprints,
        labels.reshape(steps, 1, GROUP * foot_cols),
        jnp.asarray(row_table),
        jnp.asarray(col_table),
        jnp.asarray(mix),
    )


def project_general(moved, footprints, labels, owners):
    frames, side, width = moved.shape
    base = jnp.asarray(gauss_table(side, pixel_sigma))
    time = jnp.asarray(gauss_table(frames, frame_sigma))
    blocks = moved.reshape(frames, side, width // side, side)
    dot = lambda spec, a, b: jnp.einsum(spec, a, b, preferred_element_type=jnp.float32)
    along_rows = dot("ij,fjpc->fipc", base, blocks).astype(jnp.bfloat16)
    along_cols = dot("fipc,dc->fipd", along_rows, base).astype(jnp.bfloat16)
    clean = (blocks.astype(jnp.float32) - dot("gf,fipc->gipc", time, along_cols)).astype(jnp.bfloat16)
    pixels = clean.transpose(2, 0, 1, 3).reshape(width // side, frames, side * side)
    partial = dot("pfx,pkx->fpk", pixels, footprints).reshape(frames, -1)
    wanted = jnp.arange(NEURONS, dtype=jnp.int32)
    onehot = (labels.reshape(-1)[:, None] == wanted[None, :]).astype(jnp.float32)
    sums = jnp.dot(partial, onehot, precision=lax.Precision.HIGHEST, preferred_element_type=jnp.float32)
    return sums.reshape(frames, owners, -1).transpose(1, 0, 2).reshape(owners * frames, -1)


def on_device(movie, shifts, footprints, neuron_ids):
    band = movie[0]
    before, after = halo(band)
    registered = register(band, before, after, shifts)
    rows, width = registered.shape
    groups = lax.axis_size("tm")
    owners = groups * lax.axis_size("pix")
    wide = footprints.shape[1] * PATCH
    slabs = registered.reshape(rows // PATCH, PATCH, width // wide, wide)
    slabs = slabs.transpose(0, 2, 1, 3).reshape(groups, PATCH, wide)
    moved = lax.all_to_all(slabs, "tm", split_axis=0, concat_axis=0, tiled=True)
    frames = moved.shape[0]
    fits = frames * 32 == GROUP * PATCH and wide % (GROUP * PATCH) == 0 and NEURONS // owners == LANES
    form = project if fits else project_general
    sums = form(moved, footprints[0], neuron_ids[0], owners)
    sums = lax.all_to_all(
        sums.reshape(owners, frames, -1), ("tm", "pix"), split_axis=0, concat_axis=0, tiled=True
    )
    return jnp.sum(sums, axis=0).T


def solution(mesh):
    in_specs = (
        P("tm", "pix", None),
        P("tm", "pix", None, None),
        P("pix", "tm", None, None),
        P("pix", "tm", None),
    )
    out_specs = P(("tm", "pix"), None)
    return jax.shard_map(
        on_device, mesh=mesh, in_specs=in_specs, out_specs=out_specs, check_vma=False
    )
```

```python
import jax
import jax.numpy as jnp
import ml_dtypes
import numpy as np
from jax import lax
from jax.experimental import pallas as pl
from jax.experimental.pallas import tpu as pltpu
from jax.sharding import PartitionSpec as P

TILE = 128
MAXSHIFT = 16
PATCH = 64
NEURONS = 4096
LANES = 128
GROUP = 4


pixel_sigma = 3.0
frame_sigma = 4.0


def gauss_table(count, sigma):
    places = np.arange(count).astype(np.float32)
    apart = places[:, None] - places[None, :]
    weights = np.exp(-apart * apart / np.float32(2.0 * sigma * sigma)).astype(np.float32)
    table = weights / np.sum(weights, axis=1, keepdims=True, dtype=np.float32)
    return table.astype(ml_dtypes.bfloat16)


def halo(band):
    count = lax.axis_size("pix")
    up = [(i, i + 1) for i in range(count - 1)]
    down = [(i + 1, i) for i in range(count - 1)]
    before = lax.ppermute(band[-MAXSHIFT:], "pix", up)
    after = lax.ppermute(band[:MAXSHIFT], "pix", down)
    return before, after


def register_kernel(shift_ref, band_ref, before_ref, after_ref, out_ref, padded):
    rows, width = band_ref.shape
    across = width // TILE
    tall = rows + 2 * MAXSHIFT
    for j in (0, across + 1):
        padded[j] = jnp.zeros((tall, TILE), jnp.float32)
    for j in range(across):
        lanes = pl.ds(j * TILE, TILE)
        padded[j + 1, pl.ds(0, MAXSHIFT), :] = before_ref[:, lanes].astype(jnp.float32)
        padded[j + 1, pl.ds(MAXSHIFT, rows), :] = band_ref[:, lanes].astype(jnp.float32)
        padded[j + 1, pl.ds(rows + MAXSHIFT, MAXSHIFT), :] = after_ref[:, lanes].astype(jnp.float32)

    gap = lax.broadcasted_iota(jnp.int32, (2 * TILE, TILE), 0) - lax.broadcasted_iota(
        jnp.int32, (2 * TILE, TILE), 1
    )

    @pl.loop(0, rows // TILE)
    def _(a):
        for b in range(across):
            place = (a * across + b) * 2
            dy = shift_ref[place]
            dx = shift_ref[place + 1]
            left = dx < 0
            start = jnp.where(left, b, b + 1)
            at = pl.ds(a * TILE + MAXSHIFT + dy, TILE)
            window = jnp.concatenate([padded[start, at, :], padded[start + 1, at, :]], axis=1)
            pick = (gap == jnp.where(left, dx + TILE, dx)).astype(jnp.float32).astype(jnp.bfloat16)
            moved = jnp.dot(window.astype(jnp.bfloat16), pick, preferred_element_type=jnp.float32)
            out_ref[pl.ds(pl.multiple_of(a * TILE, TILE), TILE), b * TILE : (b + 1) * TILE] = moved.astype(
                jnp.bfloat16
            )


def register(band, before, after, shifts):
    rows, width = band.shape
    vmem = pl.BlockSpec(memory_space=pltpu.VMEM)
    return pl.pallas_call(
        register_kernel,
        out_shape=jax.ShapeDtypeStruct((rows, width), jnp.bfloat16),
        in_specs=[pl.BlockSpec(memory_space=pltpu.SMEM), vmem, vmem, vmem],
        out_specs=vmem,
        scratch_shapes=[pltpu.VMEM((width // TILE + 2, rows + 2 * MAXSHIFT, TILE), jnp.float32)],
        compiler_params=pltpu.CompilerParams(vmem_limit_bytes=24 << 20),
        name="register",
    )(shifts.reshape(-1), band, before, after)


def project_step(local, x, blocks, ids, row_ref, col_ref, mix_ref):
    frames, side, cols = x.shape
    foot_cols = blocks.shape[1]
    half = row_ref.shape[0] // frames
    moved = x.reshape(frames * side, cols)
    chunk = row_ref.shape[0]
    along_rows = jnp.concatenate(
        [
            jnp.dot(row_ref[...], moved[i : i + chunk], preferred_element_type=jnp.float32)
            for i in range(0, frames * side, chunk)
        ],
        axis=0,
    ).astype(jnp.bfloat16)
    along_cols = jnp.dot(along_rows, col_ref[...], preferred_element_type=jnp.float32).astype(jnp.bfloat16)
    patches = cols // side
    low = lax.broadcasted_iota(jnp.int32, (frames, LANES), 1) < side
    pieces = [[] for _ in range(patches)]
    for h in range(side // half):
        stack = [moved[f * side + h * half : f * side + (h + 1) * half] for f in range(frames)]
        stack += [along_cols[f * side + h * half : f * side + (h + 1) * half] for f in range(frames)]
        clean = jnp.dot(mix_ref[...], jnp.concatenate(stack, axis=0), preferred_element_type=jnp.float32)
        for i in range(half // 2):
            for j in range(cols // LANES):
                first = clean[2 * i * frames : (2 * i + 1) * frames, j * LANES : (j + 1) * LANES]
                second = clean[(2 * i + 1) * frames : (2 * i + 2) * frames, j * LANES : (j + 1) * LANES]
                pieces[2 * j].append(jnp.where(low, first, pltpu.roll(second, side, 1)))
                pieces[2 * j + 1].append(jnp.where(low, pltpu.roll(first, side, 1), second))
    pixels = jnp.concatenate([jnp.concatenate(p, axis=1) for p in pieces], axis=0).astype(jnp.bfloat16)
    blocks = blocks.reshape(patches * foot_cols, side * side)
    product = lax.dot_general(pixels, blocks, (((1,), (1,)), ((), ())), preferred_element_type=jnp.float32)
    count = product.shape[1]
    owner_patch = lax.broadcasted_iota(jnp.int32, (frames, count), 1) // foot_cols
    partial = jnp.zeros((frames, count), jnp.float32)
    for p in range(patches):
        partial = jnp.where(owner_patch == p, product[p * frames : (p + 1) * frames], partial)
    owner = jnp.broadcast_to(ids // local, (frames, count))
    within = ids % local
    onehot = (
        (lax.broadcasted_iota(jnp.int32, (local, count), 0) == within).astype(jnp.float32).astype(jnp.bfloat16)
    )
    total = None
    rest = partial
    for _ in range(3):
        piece = rest.astype(jnp.bfloat16).astype(jnp.float32)
        rest = rest - piece
        spread = jnp.concatenate(
            [jnp.where(owner == o, piece, 0.0) for o in range(NEURONS // local)], axis=0
        ).astype(jnp.bfloat16)
        term = lax.dot_general(spread, onehot, (((1,), (1,)), ((), ())), preferred_element_type=jnp.float32)
        total = term if total is None else total + term
    return total


def exchange_kernel(
    local, slab_ref, foot_ref, ids_ref, row_ref, col_ref, mix_ref, out_ref, moved, feet, send, recv, here, feed
):
    groups, side, width = slab_ref.shape
    steps = ids_ref.shape[0]
    wide = width // steps
    me = lax.axis_index("tm")
    barrier = pltpu.get_barrier_semaphore()
    for d in range(1, groups):
        pl.semaphore_signal(
            barrier, inc=1, device_id={"tm": lax.rem(me + d, groups)}, device_id_type=pl.DeviceIdType.MESH
        )
    own = pltpu.make_async_copy(slab_ref.at[me], moved.at[me], here)
    own.start()

    def feet_copy(s):
        return pltpu.make_async_copy(foot_ref.at[pl.ds(s * GROUP, GROUP)], feet.at[s], feed.at[s])

    def send_copy(s, d):
        to = lax.rem(me + d, groups)
        lanes = pl.ds(pl.multiple_of(s * wide, wide), wide)
        return pltpu.make_async_remote_copy(
            src_ref=slab_ref.at[to, :, lanes],
            dst_ref=moved.at[me, :, lanes],
            send_sem=send.at[s, d - 1],
            recv_sem=recv.at[s, d - 1],
            device_id={"tm": to},
            device_id_type=pl.DeviceIdType.MESH,
        )

    pl.semaphore_wait(barrier, groups - 1)

    @pl.loop(0, steps)
    def _(s):
        for d in range(1, groups):
            send_copy(s, d).start()

    @pl.loop(0, steps)
    def _(s):
        feet_copy(s).start()

    out_ref[...] = jnp.zeros_like(out_ref)
    own.wait()

    @pl.loop(0, steps)
    def _(s):
        feet_copy(s).wait()
        for d in range(1, groups):
            send_copy(s, d).wait_recv()
        lanes = pl.ds(pl.multiple_of(s * wide, wide), wide)
        out_ref[...] += project_step(local, moved[:, :, lanes], feet[s], ids_ref[s], row_ref, col_ref, mix_ref)

    @pl.loop(0, steps)
    def _(s):
        for d in range(1, groups):
            send_copy(s, d).wait_send()


def collect_kernel(sums_ref, out_ref, landed, send, recv):
    owners = sums_ref.shape[0]
    across = lax.axis_size("pix")
    me = lax.axis_index("tm") * across + lax.axis_index("pix")
    barrier = pltpu.get_barrier_semaphore()

    def place(t):
        return {"tm": t // across, "pix": lax.rem(t, across)}

    @pl.loop(1, owners)
    def _(d):
        pl.semaphore_signal(
            barrier, inc=1, device_id=place(lax.rem(me + d, owners)), device_id_type=pl.DeviceIdType.MESH
        )

    pl.semaphore_wait(barrier, owners - 1)

    def copy(d):
        to = lax.rem(me + d, owners)
        return pltpu.make_async_remote_copy(
            src_ref=sums_ref.at[to],
            dst_ref=landed.at[me],
            send_sem=send.at[d - 1],
            recv_sem=recv.at[d - 1],
            device_id=place(to),
            device_id_type=pl.DeviceIdType.MESH,
        )

    @pl.loop(1, owners)
    def _(d):
        copy(d).start()

    landed[me] = sums_ref[me]

    @pl.loop(1, owners)
    def _(d):
        copy(d).wait_recv()

    out_ref[...] = jnp.sum(landed[...], axis=0)

    @pl.loop(1, owners)
    def _(d):
        copy(d).wait_send()


def collect(sums):
    owners, frames, local = sums.shape
    vmem = pl.BlockSpec(memory_space=pltpu.VMEM)
    return pl.pallas_call(
        collect_kernel,
        out_shape=jax.ShapeDtypeStruct((frames, local), jnp.float32),
        in_specs=[vmem],
        out_specs=vmem,
        scratch_shapes=[
            pltpu.VMEM((owners, frames, local), jnp.float32),
            pltpu.SemaphoreType.DMA((owners - 1,)),
            pltpu.SemaphoreType.DMA((owners - 1,)),
        ],
        compiler_params=pltpu.CompilerParams(collective_id=1, has_side_effects=True),
        name="collect",
    )(sums)


def exchange_project(slabs, footprints, labels, owners):
    frames, side, width = slabs.shape
    steps = width // (GROUP * side)
    foot_cols = footprints.shape[1]
    local = NEURONS // owners
    base = gauss_table(side, pixel_sigma)
    time = gauss_table(frames, frame_sigma)
    full = GROUP * side
    eye = np.eye(GROUP, dtype=np.float32)
    row_table = np.kron(eye, base.astype(np.float32)).astype(ml_dtypes.bfloat16)
    col_table = np.kron(eye, base.astype(np.float32).T).astype(ml_dtypes.bfloat16)
    half = full // frames
    spots = np.eye(half, dtype=np.float32)
    keep = np.einsum("gf,rs->rgfs", np.eye(frames, dtype=np.float32), spots)
    blur = np.einsum("gf,rs->rgfs", time.astype(np.float32), spots)
    mix = np.concatenate([keep.reshape(full, full), -blur.reshape(full, full)], axis=1).astype(ml_dtypes.bfloat16)
    vmem = pl.BlockSpec(memory_space=pltpu.VMEM)
    return pl.pallas_call(
        lambda *refs: exchange_kernel(local, *refs),
        out_shape=jax.ShapeDtypeStruct((owners * frames, local), jnp.float32),
        in_specs=[vmem, pl.BlockSpec(memory_space=pl.ANY), vmem, vmem, vmem, vmem],
        out_specs=vmem,
        scratch_shapes=[
            pltpu.VMEM((frames, side, width), jnp.bfloat16),
            pltpu.VMEM((steps, GROUP, foot_cols, side * side), jnp.bfloat16),
            pltpu.SemaphoreType.DMA((steps, frames - 1)),
            pltpu.SemaphoreType.DMA((steps, frames - 1)),
            pltpu.SemaphoreType.DMA,
            pltpu.SemaphoreType.DMA((steps,)),
        ],
        compiler_params=pltpu.CompilerParams(
            vmem_limit_bytes=44 << 20, collective_id=0, has_side_effects=True
        ),
        name="exchange_project",
    )(
        slabs,
        footprints,
        labels.reshape(steps, 1, GROUP * foot_cols),
        jnp.asarray(row_table),
        jnp.asarray(col_table),
        jnp.asarray(mix),
    )


def project_general(moved, footprints, labels, owners):
    frames, side, width = moved.shape
    base = jnp.asarray(gauss_table(side, pixel_sigma))
    time = jnp.asarray(gauss_table(frames, frame_sigma))
    blocks = moved.reshape(frames, side, width // side, side)
    dot = lambda spec, a, b: jnp.einsum(spec, a, b, preferred_element_type=jnp.float32)
    along_rows = dot("ij,fjpc->fipc", base, blocks).astype(jnp.bfloat16)
    along_cols = dot("fipc,dc->fipd", along_rows, base).astype(jnp.bfloat16)
    clean = (blocks.astype(jnp.float32) - dot("gf,fipc->gipc", time, along_cols)).astype(jnp.bfloat16)
    pixels = clean.transpose(2, 0, 1, 3).reshape(width // side, frames, side * side)
    partial = dot("pfx,pkx->fpk", pixels, footprints).reshape(frames, -1)
    wanted = jnp.arange(NEURONS, dtype=jnp.int32)
    onehot = (labels.reshape(-1)[:, None] == wanted[None, :]).astype(jnp.float32)
    sums = jnp.dot(partial, onehot, precision=lax.Precision.HIGHEST, preferred_element_type=jnp.float32)
    return sums.reshape(frames, owners, -1).transpose(1, 0, 2).reshape(owners * frames, -1)


def on_device(movie, shifts, footprints, neuron_ids):
    band = movie[0]
    before, after = halo(band)
    registered = register(band, before, after, shifts)
    rows, width = registered.shape
    groups = lax.axis_size("tm")
    owners = groups * lax.axis_size("pix")
    wide = footprints.shape[1] * PATCH
    slabs = registered.reshape(rows // PATCH, PATCH, width // wide, wide)
    slabs = slabs.transpose(0, 2, 1, 3).reshape(groups, PATCH, wide)
    frames = groups * movie.shape[0]
    fits = frames * 32 == GROUP * PATCH and wide % (GROUP * PATCH) == 0 and NEURONS // owners == LANES
    if fits:
        sums = exchange_project(slabs, footprints[0], neuron_ids[0], owners)
        return collect(sums.reshape(owners, frames, -1)).T
    moved = lax.all_to_all(slabs, "tm", split_axis=0, concat_axis=0, tiled=True)
    sums = project_general(moved, footprints[0], neuron_ids[0], owners)
    sums = lax.all_to_all(
        sums.reshape(owners, frames, -1), ("tm", "pix"), split_axis=0, concat_axis=0, tiled=True
    )
    return jnp.sum(sums, axis=0).T


def solution(mesh):
    in_specs = (
        P("tm", "pix", None),
        P("tm", "pix", None, None),
        P("pix", "tm", None, None),
        P("pix", "tm", None),
    )
    out_specs = P(("tm", "pix"), None)
    return jax.shard_map(
        on_device, mesh=mesh, in_specs=in_specs, out_specs=out_specs, check_vma=False
    )
```
